32 devices in a mesh: wall: 4 (over z), stream: 8 (over y, x, core).
Axes of the slice: x: 2, y: 2, z: 4, core: 2. Of those that a mesh axis runs over, the one named last changes fastest.
Arguments:
- state: float32 [20, 135, 2048], P('wall', None, 'stream'), may hold values from -6 to 6
- pivot_inv: float32 [20, 135, 135], P('wall'), may hold values from -0.02 to 0.2
- lower_block: float32 [20, 135, 135], P('wall'), may hold values from -22 to 1.5
- upper_block: float32 [20, 135, 135], P('wall'), may hold values from -1.2 to 0.2
- volume: float32 [135, 135], replicated, may hold values from -0.5 to 0.5
- face_minus: float32 [45, 135], replicated, may hold values from -0.5 to 0.5
- face_plus: float32 [45, 135], replicated, may hold values from -0.5 to 0.5
- lift_minus: float32 [135, 45], replicated, may hold values from -0.875 to 0.875
- lift_plus: float32 [135, 45], replicated, may hold values from -0.875 to 0.875
- offsets: int32 [2048], P('stream'), may hold values from 0 to 4
- counts: int32 [2048], P('stream'), may hold values from 10 to 15
Outputs:
- section_state: float32 [20, 135, 2048], P('wall', None, 'stream')
- section_rate: float32 [20, 135, 2048], P('wall', None, 'stream')
The draws below stay inside these ranges and needn't reach their ends.
All inputs are finite; a program needn't handle non-finite values.
Results may differ from the reference program's by a relative error of at most 0.00019.
Values sent between devices are 32-bit elements; how exact they have to be, the bound alone decides.
A program may use at most 64 MiB of HBM per device.

```python
import math
import jax
import jax.numpy as jnp
from jax import lax

B = 135
F = 45
LINE_ELEMENTS = 20
LINES = 2048


def coupling_speeds(key):
    keys = jax.random.split(key, 4)
    share = 0.5
    slow = jax.random.uniform(keys[0], (B,)) < share
    spread = jax.random.uniform(keys[1], (LINE_ELEMENTS, B), dtype=jnp.float32)
    slow_rate = jnp.exp(-(0.5 + spread) / LINE_ELEMENTS - 0.045)
    fast_rate = jnp.exp(-1.0 / (3.0 + 5.0 * spread))
    decay_speeds = jnp.where(slow[None, :], slow_rate, fast_rate)
    spike_positions = jax.random.randint(keys[2], (3,), 0, LINE_ELEMENTS)
    spike_batch = jnp.any(jnp.arange(LINE_ELEMENTS)[:, None] == spike_positions[None, :], axis=1)
    split_point = jax.random.uniform(keys[3], (LINE_ELEMENTS, 1), minval=0.5, maxval=0.8)
    return decay_speeds * jnp.where(spike_batch[:, None], split_point, 1.0)


def pivot_scale(key):
    return 0.1 * jax.random.uniform(key, (LINE_ELEMENTS, B), minval=0.7, maxval=1.4)


def off_part(key, scale):
    identity = jnp.eye(B, dtype=jnp.float32)
    noise = jax.random.truncated_normal(key, -3.0, 3.0, (LINE_ELEMENTS, B, B), dtype=jnp.float32)
    return scale * noise / math.sqrt(B) * (1.0 - identity)


def draw_pivot_inv(key, part):
    base = jax.random.fold_in(key, 11)
    diagonal = pivot_scale(jax.random.fold_in(base, 1))
    identity = jnp.eye(B, dtype=jnp.float32)
    return diagonal[:, :, None] * identity + off_part(jax.random.fold_in(base, 2), 0.022)


def draw_lower_block(key, part):
    base = jax.random.fold_in(key, 11)
    diagonal = pivot_scale(jax.random.fold_in(base, 1))
    decay_speeds = coupling_speeds(jax.random.fold_in(base, 3))
    identity = jnp.eye(B, dtype=jnp.float32)
    return (-decay_speeds / diagonal)[:, :, None] * identity + off_part(jax.random.fold_in(base, 4), 2.2)


def draw_upper_block(key, part):
    base = jax.random.fold_in(key, 29)
    decay_speeds = coupling_speeds(jax.random.fold_in(base, 1))
    identity = jnp.eye(B, dtype=jnp.float32)
    return (-decay_speeds)[:, :, None] * identity + off_part(jax.random.fold_in(base, 2), 0.22)


def place_ends(entries, rng, low, largest):
    extent = entries.shape
    spot = [jax.random.randint(jax.random.fold_in(rng, axis), (), 0, extent[axis]) for axis in range(len(extent))]
    entries = entries.at[tuple(spot)].set(low)
    longest = extent.index(max(extent))
    spot[longest] = (spot[longest] + 1) % extent[longest]
    return entries.at[tuple(spot)].set(largest)


def block_scale(rng, extent, pieces, low, high):
    def one(axis_at, parts):
        steps = jax.random.uniform(jax.random.fold_in(jax.random.fold_in(rng, 6), axis_at), (parts,), jnp.float32, low / len(pieces), high / len(pieces))
        return jnp.repeat(jnp.exp(steps), extent[axis_at] // parts).reshape((-1,) + (1,) * (len(extent) - axis_at - 1))

    loudness = one(*pieces[0])
    for cut in pieces[1:]:
        loudness = loudness * one(*cut)
    return loudness


def gaussian(key, shape, width, reach, cuts=(), kind=jnp.bfloat16):
    result = jax.random.normal(key, shape, jnp.float32) * width
    if len(cuts) > 0:
        result = block_scale(key, shape, cuts, -0.22, 0.18) * result
    return jnp.clip(result, min=-reach, max=reach).astype(kind)


def setup_inputs(seed: int = 0) -> dict:
    seeds = jax.random.split(jax.random.key(seed), 12)
    return {
        "state": gaussian(seeds[0], (LINE_ELEMENTS, B, LINES), 1.0, 6.0, ((0, 4), (2, 8)), jnp.float32),
        "pivot_inv": draw_pivot_inv(jax.random.fold_in(seeds[11], 71), 0),
        "lower_block": draw_lower_block(jax.random.fold_in(seeds[11], 71), 0),
        "upper_block": draw_upper_block(jax.random.fold_in(seeds[11], 71), 0),
        "volume": gaussian(seeds[4], (B, B), B ** -0.5, 0.5, (), jnp.float32),
        "face_minus": gaussian(seeds[5], (F, B), B ** -0.5, 0.5, (), jnp.float32),
        "face_plus": gaussian(seeds[6], (F, B), B ** -0.5, 0.5, (), jnp.float32),
        "lift_minus": gaussian(seeds[7], (B, F), F ** -0.5, 0.875, (), jnp.float32),
        "lift_plus": gaussian(seeds[8], (B, F), F ** -0.5, 0.875, (), jnp.float32),
        "offsets": place_ends(jax.random.randint(seeds[9], (LINES,), 0, LINE_ELEMENTS // 4), jax.random.fold_in(seeds[9], 1), 0, (LINE_ELEMENTS // 4) - 1).astype(jnp.int32),
        "counts": place_ends(jax.random.randint(seeds[10], (LINES,), LINE_ELEMENTS // 2, LINE_ELEMENTS - LINE_ELEMENTS // 4 + 1), jax.random.fold_in(seeds[10], 1), LINE_ELEMENTS // 2, (LINE_ELEMENTS - LINE_ELEMENTS // 4 + 1) - 1).astype(jnp.int32),
    }


section_step = 0.4


def matmul(left, right):
    return jnp.dot(left, right, precision=lax.Precision.HIGHEST)


def element_rate(field, volume, face_minus, face_plus, lift_minus, lift_plus):
    low = matmul(face_minus, field)
    high = matmul(face_plus, field)
    jump_up = jnp.roll(low, -1, axis=1) - high
    jump_down = jnp.roll(jump_up, 1, axis=1)
    return matmul(volume, field) + matmul(lift_plus, jump_up) + matmul(lift_minus, jump_down)


def reference(state, pivot_inv, lower_block, upper_block, volume, face_minus, face_plus, lift_minus, lift_plus, offsets, counts):
    element = jnp.arange(LINE_ELEMENTS, dtype=jnp.int32)[:, None]
    active = ((offsets[None, :] <= element) & (element < offsets[None, :] + counts[None, :])).astype(state.dtype)
    zero_rows = jnp.zeros((B, state.shape[2]), state.dtype)

    def forward(previous, items):
        field, pivot, below, keep = items
        right_side = keep[None, :] * (field + section_step * element_rate(field, volume, face_minus, face_plus, lift_minus, lift_plus))
        current = matmul(pivot, right_side - matmul(below, previous))
        return current, current

    unused, forward_rows = lax.scan(forward, zero_rows, (state, pivot_inv, lower_block, active))

    def backward(after, items):
        row_now, above = items
        current = row_now - matmul(above, after)
        return current, current

    ignored_second, solution = lax.scan(backward, zero_rows, (forward_rows, upper_block), reverse=True)
    section_state = active[:, None, :] * solution

    def rate_of(pair):
        return pair[1][None, :] * element_rate(pair[0], volume, face_minus, face_plus, lift_minus, lift_plus)

    section_rate = lax.map(rate_of, (section_state, active))
    return section_state, section_rate
```

```python
import functools

import jax
import jax.numpy as jnp
from jax import lax
from jax.experimental import pallas as pl
from jax.experimental.pallas import tpu as pltpu
from jax.sharding import PartitionSpec as P

section_step = 0.4
MESH = pl.DeviceIdType.MESH
F32 = jnp.float32
BF16 = jnp.bfloat16


def ceil_to(size, unit):
    return (size + unit - 1) // unit * unit


def split(x):
    high = x.astype(BF16)
    return high, (x - high.astype(F32)).astype(BF16)


def dot(a, b):
    return jnp.dot(a, b, preferred_element_type=F32)


def product(matrix, x):
    high, low = matrix
    x_high, x_low = split(x)
    return dot(high, x_high) + (dot(low, x_high) + dot(high, x_low))


def kernel(
    walls,
    streams,
    state,
    pivot_inv,
    lower_block,
    upper_block,
    volume,
    face_minus,
    face_plus,
    lift_minus,
    lift_plus,
    offsets,
    counts,
    out_state,
    out_rate,
    trace_m,
    lift_m,
    step_m,
    upper_m,
    reach_y,
    reach_x,
    exit_m,
    traces,
    rows,
    halo_out,
    halo_in,
    y_out,
    y_in,
    x_out,
    x_in,
    halo_send,
    halo_recv,
    y_send,
    y_recv,
    x_send,
    x_recv,
):
    elements, size, lines = state.shape
    faces = face_minus.shape[0]
    size_pad, face_pad = ceil_to(size, 16), ceil_to(faces, 16)
    chunks = y_out.shape[0]
    width = lines // chunks
    position = lax.axis_index("wall")
    here = lax.axis_index("stream")
    right, left = lax.rem(here + 1, streams), lax.rem(here + streams - 1, streams)

    barrier = pltpu.get_barrier_semaphore()
    pl.semaphore_signal(barrier, inc=1, device_id={"stream": left}, device_id_type=MESH)
    pl.semaphore_signal(barrier, inc=1, device_id={"stream": right}, device_id_type=MESH)

    @pl.when(position > 0)
    def _():
        pl.semaphore_signal(barrier, inc=1, device_id={"wall": position - 1}, device_id_type=MESH)

    @pl.when(position < walls - 1)
    def _():
        pl.semaphore_signal(barrier, inc=1, device_id={"wall": position + 1}, device_id_type=MESH)

    inner = jnp.logical_and(position > 0, position < walls - 1)

    @pl.when(inner)
    def _():
        pl.semaphore_wait(barrier, 4)

    @pl.when(jnp.logical_not(inner))
    def _():
        pl.semaphore_wait(barrier, 3)

    def put(ref, index, value):
        high, low = split(value)
        ref[0, index] = high
        ref[1, index] = low

    def take(ref, index):
        return ref[0, index], ref[1, index]

    trace_m[...] = jnp.zeros_like(trace_m)
    lift_m[...] = jnp.zeros_like(lift_m)
    for first, ref in ((0, volume), (size_pad, face_minus), (size_pad + face_pad, face_plus)):
        high, low = split(ref[...])
        trace_m[0, first : first + ref.shape[0], :] = high
        trace_m[1, first : first + ref.shape[0], :] = low
    for which, ref in ((0, lift_plus), (1, lift_minus)):
        high, low = split(ref[...])
        lift_m[0, which, :, :faces] = high
        lift_m[1, which, :, :faces] = low

    lane = lax.broadcasted_iota(jnp.int32, (face_pad, lines), 1)
    narrow = lax.broadcasted_iota(jnp.int32, (face_pad, halo_out.shape[2]), 1)

    def halo_copy(turn, side):
        slot = 2 * turn + side
        return pltpu.make_async_remote_copy(
            src_ref=halo_out.at[slot],
            dst_ref=halo_in.at[slot],
            send_sem=halo_send.at[slot],
            recv_sem=halo_recv.at[slot],
            device_id={"stream": left if side == 0 else right},
            device_id_type=MESH,
        )

    def start_rate(field, turn):
        first = jnp.zeros((face_pad, halo_out.shape[2]), F32)
        last = jnp.zeros((face_pad, halo_out.shape[2]), F32)
        for k in range(elements):
            out = product((trace_m[0], trace_m[1]), field(k))
            traces[k] = out
            low = out[size_pad : size_pad + face_pad]
            high = out[size_pad + face_pad :]
            first = jnp.where(narrow == k, low[:, :1], first)
            last = jnp.where(narrow == k, high[:, lines - 1 :], last)
        halo_out[2 * turn] = first
        halo_out[2 * turn + 1] = last
        halo_copy(turn, 0).start()
        halo_copy(turn, 1).start()

    def wait_rate(turn):
        halo_copy(turn, 0).wait()
        halo_copy(turn, 1).wait()

    def rate(k, turn):
        low = traces[k, size_pad : size_pad + face_pad, :]
        high = traces[k, size_pad + face_pad :, :]
        low_next = halo_in[2 * turn][:, k : k + 1]
        high_prev = halo_in[2 * turn + 1][:, k : k + 1]
        up = jnp.where(lane == lines - 1, low_next, pltpu.roll(low, lines - 1, 1)) - high
        down = low - jnp.where(lane == 0, high_prev, pltpu.roll(high, 1, 1))
        return (
            traces[k, :size, :]
            + product((lift_m[0, 0], lift_m[1, 0]), up)
            + product((lift_m[0, 1], lift_m[1, 1]), down)
        )

    begin = offsets[...]
    end = begin + counts[...]

    def active(k):
        element = position * elements + k
        return ((begin <= element) & (element < end)).astype(F32)

    start_rate(lambda k: state[k], 0)

    for k in range(elements):
        step = product(split(pivot_inv[k]), lower_block[k])
        put(step_m, k, step)
        put(upper_m, k, upper_block[k])
    spikes = [-(step_m[0, 0].astype(F32) + step_m[1, 0].astype(F32))]
    for k in range(1, elements):
        spikes.append(-product(take(step_m, k), spikes[-1]))
    put(exit_m, 0, spikes[-1])
    map_y, map_x = spikes[-1], -upper_block[elements - 1]
    put(reach_y, elements - 1, map_y)
    put(reach_x, elements - 1, map_x)
    for k in reversed(range(elements - 1)):
        map_y = spikes[k] - product(take(upper_m, k), map_y)
        map_x = -product(take(upper_m, k), map_x)
        put(reach_y, k, map_y)
        put(reach_x, k, map_x)

    wait_rate(0)
    local = None
    for k in range(elements):
        right_side = active(k) * (state[k] + section_step * rate(k, 0))
        forced = product(split(pivot_inv[k]), right_side)
        local = forced if k == 0 else forced - product(take(step_m, k), local)
        rows[k] = local

    def y_copy(c):
        return pltpu.make_async_remote_copy(
            src_ref=y_out.at[c],
            dst_ref=y_in.at[c],
            send_sem=y_send.at[c],
            recv_sem=y_recv.at[c],
            device_id={"wall": lax.rem(position + 1, walls)},
            device_id_type=MESH,
        )

    def x_copy(c):
        return pltpu.make_async_remote_copy(
            src_ref=x_out.at[c],
            dst_ref=x_in.at[c],
            send_sem=x_send.at[c],
            recv_sem=x_recv.at[c],
            device_id={"wall": lax.rem(position + walls - 1, walls)},
            device_id_type=MESH,
        )

    columns = [slice(c * width, (c + 1) * width) for c in range(chunks)]

    @pl.when(position == 0)
    def _():
        for c in range(chunks):
            y_out[c] = rows[elements - 1, :, columns[c]]
            y_copy(c).start()
            y_in[c] = jnp.zeros_like(y_in[c])

    @pl.when(position == walls - 1)
    def _():
        for c in range(chunks):
            x_in[c] = jnp.zeros_like(x_in[c])

    last_rows = [rows[elements - 1, :, columns[c]] for c in range(chunks)]
    after = rows[elements - 1]
    for k in reversed(range(elements - 1)):
        after = rows[k] - product(take(upper_m, k), after)
        rows[k] = after

    for c in range(chunks):

        @pl.when(position > 0)
        def _():
            y_copy(c).wait_recv()

            @pl.when(position < walls - 1)
            def _():
                y_out[c] = last_rows[c] + product(take(exit_m, 0), y_in[c])
                y_copy(c).start()

        @pl.when(position == walls - 1)
        def _():
            x_out[c] = rows[0, :, columns[c]] + product(take(reach_y, 0), y_in[c])
            x_copy(c).start()

    for c in range(chunks):
        for k in range(elements):
            rows[k, :, columns[c]] = rows[k, :, columns[c]] + product(take(reach_y, k), y_in[c])

    for c in range(chunks):

        @pl.when(position < walls - 1)
        def _():
            x_copy(c).wait_recv()

            @pl.when(position > 0)
            def _():
                x_out[c] = rows[0, :, columns[c]] + product(take(reach_x, 0), x_in[c])
                x_copy(c).start()

    for k in range(elements):
        for c in range(chunks):
            solved = rows[k, :, columns[c]] + product(take(reach_x, k), x_in[c])
            out_state[k, :, columns[c]] = active(k)[:, columns[c]] * solved

    start_rate(lambda k: out_state[k], 1)

    @pl.when(position < walls - 1)
    def _():
        for c in range(chunks):
            y_copy(c).wait_send()

    @pl.when(position > 0)
    def _():
        for c in range(chunks):
            x_copy(c).wait_send()

    wait_rate(1)
    for k in range(elements):
        out_rate[k] = active(k) * rate(k, 1)


def solution(mesh):
    walls, streams = mesh.shape["wall"], mesh.shape["stream"]

    def body(
        state,
        pivot_inv,
        lower_block,
        upper_block,
        volume,
        face_minus,
        face_plus,
        lift_minus,
        lift_plus,
        offsets,
        counts,
    ):
        elements, size, lines = state.shape
        faces = face_minus.shape[0]
        size_pad, face_pad = ceil_to(size, 16), ceil_to(faces, 16)
        chunks = 2 if lines % 256 == 0 else 1
        width = lines // chunks
        halo_width = ceil_to(elements, 128)
        vmem = pl.BlockSpec(memory_space=pltpu.VMEM)
        return pl.pallas_call(
            functools.partial(kernel, walls, streams),
            out_shape=(jax.ShapeDtypeStruct(state.shape, F32),) * 2,
            in_specs=[vmem] * 11,
            out_specs=(vmem, vmem),
            scratch_shapes=[
                pltpu.VMEM((2, size_pad + 2 * face_pad, size), BF16),
                pltpu.VMEM((2, 2, size, face_pad), BF16),
                pltpu.VMEM((2, elements, size, size), BF16),
                pltpu.VMEM((2, elements, size, size), BF16),
                pltpu.VMEM((2, elements, size, size), BF16),
                pltpu.VMEM((2, elements, size, size), BF16),
                pltpu.VMEM((2, 1, size, size), BF16),
                pltpu.VMEM((elements, size_pad + 2 * face_pad, lines), F32),
                pltpu.VMEM((elements, size, lines), F32),
                pltpu.VMEM((4, face_pad, halo_width), F32),
                pltpu.VMEM((4, face_pad, halo_width), F32),
                pltpu.VMEM((chunks, size, width), F32),
                pltpu.VMEM((chunks, size, width), F32),
                pltpu.VMEM((chunks, size, width), F32),
                pltpu.VMEM((chunks, size, width), F32),
                pltpu.SemaphoreType.DMA((4,)),
                pltpu.SemaphoreType.DMA((4,)),
                pltpu.SemaphoreType.DMA((chunks,)),
                pltpu.SemaphoreType.DMA((chunks,)),
                pltpu.SemaphoreType.DMA((chunks,)),
                pltpu.SemaphoreType.DMA((chunks,)),
            ],
            compiler_params=pltpu.CompilerParams(
                collective_id=0, has_side_effects=True, vmem_limit_bytes=32 * 1024 * 1024
            ),
        )(
            state,
            pivot_inv,
            lower_block,
            upper_block,
            volume,
            face_minus,
            face_plus,
            lift_minus,
            lift_plus,
            offsets.reshape(1, lines),
            counts.reshape(1, lines),
        )

    in_specs = (
        P("wall", None, "stream"),
        P("wall", None, None),
        P("wall", None, None),
        P("wall", None, None),
        P(),
        P(),
        P(),
        P(),
        P(),
        P("stream"),
        P("stream"),
    )
    out_specs = (P("wall", None, "stream"), P("wall", None, "stream"))
    return jax.shard_map(body, mesh=mesh, in_specs=in_specs, out_specs=out_specs, check_vma=False)
```

```python
import functools

import jax
import jax.numpy as jnp
from jax import lax
from jax.experimental import pallas as pl
from jax.experimental.pallas import tpu as pltpu
from jax.sharding import PartitionSpec as P

section_step = 0.4
MESH = pl.DeviceIdType.MESH
F32 = jnp.float32
BF16 = jnp.bfloat16


def ceil_to(size, unit):
    return (size + unit - 1) // unit * unit


def split(x):
    high = x.astype(BF16)
    return high, (x - high.astype(F32)).astype(BF16)


def dot(a, b):
    return jnp.dot(a, b, preferred_element_type=F32)


def product(matrix, x):
    high, low = matrix
    x_high, x_low = split(x)
    return dot(high, x_high) + (dot(low, x_high) + dot(high, x_low))


def kernel(
    walls,
    streams,
    state_hbm,
    pivot_hbm,
    lower_hbm,
    upper_hbm,
    volume_hbm,
    minus_hbm,
    plus_hbm,
    lift_minus_hbm,
    lift_plus_hbm,
    offsets_hbm,
    counts_hbm,
    out_state,
    out_rate,
    state,
    pivot_inv,
    lower_block,
    upper_block,
    volume,
    face_minus,
    face_plus,
    lift_minus,
    lift_plus,
    offsets,
    counts,
    load_sem,
    trace_m,
    lift_m,
    step_m,
    upper_m,
    reach_y,
    reach_x,
    exit_m,
    traces,
    rows,
    halo_out,
    halo_in,
    y_out,
    y_in,
    x_out,
    x_in,
    last,
    m_out,
    m_in,
    down_m,
    halo_send,
    halo_recv,
    y_send,
    y_recv,
    x_send,
    x_recv,
    m_send,
    m_recv,
):
    elements, size, lines = state.shape
    faces = face_minus.shape[0]
    size_pad, face_pad = ceil_to(size, 16), ceil_to(faces, 16)
    chunks = y_out.shape[0]
    width = lines // chunks
    position = lax.axis_index("wall")
    here = lax.axis_index("stream")
    right, left = lax.rem(here + 1, streams), lax.rem(here + streams - 1, streams)

    half = walls // 2
    sources = (
        (volume_hbm, volume),
        (minus_hbm, face_minus),
        (plus_hbm, face_plus),
        (state_hbm, state),
        (pivot_hbm, pivot_inv),
        (lower_hbm, lower_block),
        (upper_hbm, upper_block),
        (lift_minus_hbm, lift_minus),
        (lift_plus_hbm, lift_plus),
        (offsets_hbm, offsets),
        (counts_hbm, counts),
    )
    loads = [
        pltpu.make_async_copy(source, target, load_sem.at[i])
        for i, (source, target) in enumerate(sources)
    ]
    for load in loads:
        load.start()

    barrier = pltpu.get_barrier_semaphore()
    pl.semaphore_signal(barrier, inc=1, device_id={"stream": left}, device_id_type=MESH)
    pl.semaphore_signal(barrier, inc=1, device_id={"stream": right}, device_id_type=MESH)

    @pl.when(position > 0)
    def _():
        pl.semaphore_signal(barrier, inc=1, device_id={"wall": position - 1}, device_id_type=MESH)

    @pl.when(position < walls - 1)
    def _():
        pl.semaphore_signal(barrier, inc=1, device_id={"wall": position + 1}, device_id_type=MESH)

    inner = jnp.logical_and(position > 0, position < walls - 1)

    @pl.when(inner)
    def _():
        pl.semaphore_wait(barrier, 4)

    @pl.when(jnp.logical_not(inner))
    def _():
        pl.semaphore_wait(barrier, 3)

    def put(ref, index, value):
        high, low = split(value)
        ref[0, index] = high
        ref[1, index] = low

    def take(ref, index):
        return ref[0, index], ref[1, index]

    trace_m[...] = jnp.zeros_like(trace_m)
    lift_m[...] = jnp.zeros_like(lift_m)
    for load in loads[:3]:
        load.wait()
    for first, ref in ((0, volume), (size_pad, face_minus), (size_pad + face_pad, face_plus)):
        high, low = split(ref[...])
        trace_m[0, first : first + ref.shape[0], :] = high
        trace_m[1, first : first + ref.shape[0], :] = low
    lane = lax.broadcasted_iota(jnp.int32, (face_pad, lines), 1)
    narrow = lax.broadcasted_iota(jnp.int32, (face_pad, halo_out.shape[2]), 1)

    def halo_copy(turn, side):
        slot = 2 * turn + side
        return pltpu.make_async_remote_copy(
            src_ref=halo_out.at[slot],
            dst_ref=halo_in.at[slot],
            send_sem=halo_send.at[slot],
            recv_sem=halo_recv.at[slot],
            device_id={"stream": left if side == 0 else right},
            device_id_type=MESH,
        )

    def start_rate(field, turn):
        first = jnp.zeros((face_pad, halo_out.shape[2]), F32)
        final = jnp.zeros((face_pad, halo_out.shape[2]), F32)
        for k in range(elements):
            out = product((trace_m[0], trace_m[1]), field(k))
            traces[k] = out
            low = out[size_pad : size_pad + face_pad]
            high = out[size_pad + face_pad :]
            first = jnp.where(narrow == k, low[:, :1], first)
            final = jnp.where(narrow == k, high[:, lines - 1 :], final)
        halo_out[2 * turn] = first
        halo_out[2 * turn + 1] = final
        halo_copy(turn, 0).start()
        halo_copy(turn, 1).start()

    def wait_rate(turn):
        halo_copy(turn, 0).wait()
        halo_copy(turn, 1).wait()

    def rate(k, turn):
        low = traces[k, size_pad : size_pad + face_pad, :]
        high = traces[k, size_pad + face_pad :, :]
        low_next = halo_in[2 * turn][:, k : k + 1]
        high_prev = halo_in[2 * turn + 1][:, k : k + 1]
        up = jnp.where(lane == lines - 1, low_next, pltpu.roll(low, lines - 1, 1)) - high
        down = low - jnp.where(lane == 0, high_prev, pltpu.roll(high, 1, 1))
        return (
            traces[k, :size, :]
            + product((lift_m[0, 0], lift_m[1, 0]), up)
            + product((lift_m[0, 1], lift_m[1, 1]), down)
        )


    def active(k):
        element = position * elements + k
        return ((begin <= element) & (element < end)).astype(F32)

    loads[3].wait()
    start_rate(lambda k: state[k], 0)
    for load in loads[4:]:
        load.wait()
    begin = offsets[...]
    end = begin + counts[...]
    for which, ref in ((0, lift_plus), (1, lift_minus)):
        high, low = split(ref[...].T)
        lift_m[0, which, :, :faces] = high
        lift_m[1, which, :, :faces] = low

    for k in range(elements):
        step = product(split(pivot_inv[k]), lower_block[k])
        put(step_m, k, step)
        put(upper_m, k, upper_block[k])
    spikes = [-(step_m[0, 0].astype(F32) + step_m[1, 0].astype(F32))]
    for k in range(1, elements):
        spikes.append(-product(take(step_m, k), spikes[-1]))
    put(exit_m, 0, spikes[-1])
    map_y, map_x = spikes[-1], -upper_block[elements - 1]
    put(reach_y, elements - 1, map_y)
    put(reach_x, elements - 1, map_x)
    for k in reversed(range(elements - 1)):
        map_y = spikes[k] - product(take(upper_m, k), map_y)
        map_x = -product(take(upper_m, k), map_x)
        put(reach_y, k, map_y)
        put(reach_x, k, map_x)

    def m_copy():
        return pltpu.make_async_remote_copy(
            src_ref=m_out,
            dst_ref=m_in,
            send_sem=m_send,
            recv_sem=m_recv,
            device_id={"wall": lax.rem(position + walls - 1, walls)},
            device_id_type=MESH,
        )

    @pl.when(position == walls - 1)
    def _():
        m_out[...] = map_y
        m_copy().start()

    wait_rate(0)
    local = None
    for k in range(elements):
        right_side = active(k) * (state[k] + section_step * rate(k, 0))
        forced = product(split(pivot_inv[k]), right_side)
        local = forced if k == 0 else forced - product(take(step_m, k), local)
        rows[k] = local

    def y_copy(c):
        return pltpu.make_async_remote_copy(
            src_ref=y_out.at[c],
            dst_ref=y_in.at[c],
            send_sem=y_send.at[c],
            recv_sem=y_recv.at[c],
            device_id={"wall": lax.rem(position + 1, walls)},
            device_id_type=MESH,
        )

    def x_copy(c):
        return pltpu.make_async_remote_copy(
            src_ref=x_out.at[c],
            dst_ref=x_in.at[c],
            send_sem=x_send.at[c],
            recv_sem=x_recv.at[c],
            device_id={"wall": lax.rem(position + walls - 1, walls)},
            device_id_type=MESH,
        )

    columns = [slice(c * width, (c + 1) * width) for c in range(chunks)]

    @pl.when(position == 0)
    def _():
        for c in range(chunks):
            y_out[c] = rows[elements - 1, :, columns[c]]
            y_copy(c).start()

    last[...] = rows[elements - 1]
    after = rows[elements - 1]
    for k in reversed(range(elements - 1)):
        after = rows[k] - product(take(upper_m, k), after)
        rows[k] = after

    @pl.when(position == walls - 1)
    def _():
        for c in range(chunks):
            x_out[c] = rows[0, :, columns[c]]
            x_copy(c).start()

    @pl.when(jnp.logical_and(position >= half, position < walls - 1))
    def _():
        m_copy().wait_recv()
        through = product(take(reach_x, 0), m_in[...])
        put(down_m, 0, through)
        m_out[...] = (reach_y[0, 0].astype(F32) + reach_y[1, 0].astype(F32)) + product(
            take(down_m, 0), spikes[-1]
        )
        m_copy().start()
        above = rows[0] + product(take(down_m, 0), last[...])
        for c in range(chunks):
            x_copy(c).wait_recv()
            x_out[c] = above[:, columns[c]] + product(take(reach_x, 0), x_in[c])
            x_copy(c).start()

    @pl.when(jnp.logical_and(position > 0, position < half))
    def _():
        for c in range(chunks):
            y_copy(c).wait_recv()
            y_out[c] = last[:, columns[c]] + product(take(exit_m, 0), y_in[c])
            y_copy(c).start()

    @pl.when(position >= half)
    def _():
        for c in range(chunks):
            y_copy(c).wait_recv()

            @pl.when(position < walls - 1)
            def _():
                y_out[c] = last[:, columns[c]] + product(take(exit_m, 0), y_in[c])
                y_copy(c).start()
                x_in[c] = x_in[c] + product(split(m_in[...]), y_out[c])

    @pl.when(position == half - 1)
    def _():
        m_copy().wait_recv()
        for c in range(chunks):
            met = product(split(m_in[...]), y_out[c])
            x_copy(c).wait_recv()
            x_in[c] = x_in[c] + met

            @pl.when(position > 0)
            def _():
                x_out[c] = (
                    rows[0, :, columns[c]]
                    + product(take(reach_y, 0), y_in[c])
                    + product(take(reach_x, 0), x_in[c])
                )
                x_copy(c).start()

    @pl.when(position > 0)
    def _():
        for c in range(chunks):
            for k in range(elements):
                rows[k, :, columns[c]] += product(take(reach_y, k), y_in[c])

    @pl.when(position < half - 1)
    def _():
        for c in range(chunks):
            x_copy(c).wait_recv()

            @pl.when(position > 0)
            def _():
                x_out[c] = rows[0, :, columns[c]] + product(take(reach_x, 0), x_in[c])
                x_copy(c).start()

    @pl.when(position < walls - 1)
    def _():
        for c in range(chunks):
            for k in range(elements):
                rows[k, :, columns[c]] += product(take(reach_x, k), x_in[c])

    for k in range(elements):
        out_state[k] = active(k) * rows[k]

    start_rate(lambda k: out_state[k], 1)

    @pl.when(position < walls - 1)
    def _():
        for c in range(chunks):
            y_copy(c).wait_send()

    @pl.when(position > 0)
    def _():
        for c in range(chunks):
            x_copy(c).wait_send()

    @pl.when(position >= half)
    def _():
        m_copy().wait_send()

    wait_rate(1)
    for k in range(elements):
        out_rate[k] = active(k) * rate(k, 1)


def solution(mesh):
    walls, streams = mesh.shape["wall"], mesh.shape["stream"]

    def body(
        state,
        pivot_inv,
        lower_block,
        upper_block,
        volume,
        face_minus,
        face_plus,
        lift_minus,
        lift_plus,
        offsets,
        counts,
    ):
        elements, size, lines = state.shape
        faces = face_minus.shape[0]
        size_pad, face_pad = ceil_to(size, 16), ceil_to(faces, 16)
        chunks = 2 if lines % 256 == 0 else 1
        width = lines // chunks
        halo_width = ceil_to(elements, 128)
        vmem = pl.BlockSpec(memory_space=pltpu.VMEM)
        operands = (
            state,
            pivot_inv,
            lower_block,
            upper_block,
            volume,
            face_minus,
            face_plus,
            lift_minus.T,
            lift_plus.T,
            offsets.reshape(1, lines),
            counts.reshape(1, lines),
        )
        return pl.pallas_call(
            functools.partial(kernel, walls, streams),
            out_shape=(jax.ShapeDtypeStruct(state.shape, F32),) * 2,
            in_specs=[pl.BlockSpec(memory_space=pltpu.HBM)] * 11,
            out_specs=(vmem, vmem),
            scratch_shapes=[pltpu.VMEM(x.shape, x.dtype) for x in operands]
            + [
                pltpu.SemaphoreType.DMA((len(operands),)),
                pltpu.VMEM((2, size_pad + 2 * face_pad, size), BF16),
                pltpu.VMEM((2, 2, size, face_pad), BF16),
                pltpu.VMEM((2, elements, size, size), BF16),
                pltpu.VMEM((2, elements, size, size), BF16),
                pltpu.VMEM((2, elements, size, size), BF16),
                pltpu.VMEM((2, elements, size, size), BF16),
                pltpu.VMEM((2, 1, size, size), BF16),
                pltpu.VMEM((elements, size_pad + 2 * face_pad, lines), F32),
                pltpu.VMEM((elements, size, lines), F32),
                pltpu.VMEM((4, face_pad, halo_width), F32),
                pltpu.VMEM((4, face_pad, halo_width), F32),
                pltpu.VMEM((chunks, size, width), F32),
                pltpu.VMEM((chunks, size, width), F32),
                pltpu.VMEM((chunks, size, width), F32),
                pltpu.VMEM((chunks, size, width), F32),
                pltpu.VMEM((size, lines), F32),
                pltpu.VMEM((size, size), F32),
                pltpu.VMEM((size, size), F32),
                pltpu.VMEM((2, 1, size, size), BF16),
                pltpu.SemaphoreType.DMA((4,)),
                pltpu.SemaphoreType.DMA((4,)),
                pltpu.SemaphoreType.DMA((chunks,)),
                pltpu.SemaphoreType.DMA((chunks,)),
                pltpu.SemaphoreType.DMA((chunks,)),
                pltpu.SemaphoreType.DMA((chunks,)),
                pltpu.SemaphoreType.DMA,
                pltpu.SemaphoreType.DMA,
            ],
            compiler_params=pltpu.CompilerParams(
                collective_id=0, has_side_effects=True, vmem_limit_bytes=32 * 1024 * 1024
            ),
        )(*operands)

    in_specs = (
        P("wall", None, "stream"),
        P("wall", None, None),
        P("wall", None, None),
        P("wall", None, None),
        P(),
        P(),
        P(),
        P(),
        P(),
        P("stream"),
        P("stream"),
    )
    out_specs = (P("wall", None, "stream"), P("wall", None, "stream"))
    return jax.shard_map(body, mesh=mesh, in_specs=in_specs, out_specs=out_specs, check_vma=False)
```

```python
import functools

import jax
import jax.numpy as jnp
from jax import lax
from jax.experimental import pallas as pl
from jax.experimental.pallas import tpu as pltpu
from jax.sharding import PartitionSpec as P

section_step = 0.4
MESH = pl.DeviceIdType.MESH
F32 = jnp.float32
BF16 = jnp.bfloat16


def ceil_to(size, unit):
    return (size + unit - 1) // unit * unit


def split(x):
    high = x.astype(BF16)
    return high, (x - high.astype(F32)).astype(BF16)


def dot(a, b):
    return jnp.dot(a, b, preferred_element_type=F32)


def product(matrix, x):
    high, low = matrix
    x_high, x_low = split(x)
    return dot(high, x_high) + (dot(low, x_high) + dot(high, x_low))


def kernel(
    walls,
    streams,
    state_hbm,
    pivot_hbm,
    lower_hbm,
    upper_hbm,
    volume_hbm,
    minus_hbm,
    plus_hbm,
    lift_minus_hbm,
    lift_plus_hbm,
    offsets_hbm,
    counts_hbm,
    state_out,
    rate_out,
    state,
    pivot_inv,
    lower_block,
    upper_block,
    volume,
    face_minus,
    face_plus,
    lift_minus,
    lift_plus,
    offsets,
    counts,
    load_sem,
    store_sem,
    trace_m,
    lift_m,
    step_m,
    upper_m,
    reach_y,
    reach_x,
    exit_m,
    traces,
    rows,
    halo_out,
    halo_in,
    y_out,
    y_in,
    x_out,
    x_in,
    last,
    m_out,
    m_in,
    down_m,
    halo_send,
    halo_recv,
    y_send,
    y_recv,
    x_send,
    x_recv,
    m_send,
    m_recv,
):
    elements, size, lines = state.shape
    faces = face_minus.shape[0]
    size_pad, face_pad = ceil_to(size, 16), ceil_to(faces, 16)
    chunks = y_out.shape[0]
    width = lines // chunks
    position = lax.axis_index("wall")
    here = lax.axis_index("stream")
    right, left = lax.rem(here + 1, streams), lax.rem(here + streams - 1, streams)

    half = walls // 2
    sources = (
        (volume_hbm, volume),
        (minus_hbm, face_minus),
        (plus_hbm, face_plus),
        (state_hbm, state),
        (pivot_hbm, pivot_inv),
        (lower_hbm, lower_block),
        (upper_hbm, upper_block),
        (lift_minus_hbm, lift_minus),
        (lift_plus_hbm, lift_plus),
        (offsets_hbm, offsets),
        (counts_hbm, counts),
    )
    loads = [
        pltpu.make_async_copy(source, target, load_sem.at[i])
        for i, (source, target) in enumerate(sources)
    ]
    for load in loads:
        load.start()

    barrier = pltpu.get_barrier_semaphore()
    pl.semaphore_signal(barrier, inc=1, device_id={"stream": left}, device_id_type=MESH)
    pl.semaphore_signal(barrier, inc=1, device_id={"stream": right}, device_id_type=MESH)

    @pl.when(position > 0)
    def _():
        pl.semaphore_signal(barrier, inc=1, device_id={"wall": position - 1}, device_id_type=MESH)

    @pl.when(position < walls - 1)
    def _():
        pl.semaphore_signal(barrier, inc=1, device_id={"wall": position + 1}, device_id_type=MESH)

    inner = jnp.logical_and(position > 0, position < walls - 1)

    @pl.when(inner)
    def _():
        pl.semaphore_wait(barrier, 4)

    @pl.when(jnp.logical_not(inner))
    def _():
        pl.semaphore_wait(barrier, 3)

    def put(ref, index, value):
        high, low = split(value)
        ref[0, index] = high
        ref[1, index] = low

    def take(ref, index):
        return ref[0, index], ref[1, index]

    trace_m[...] = jnp.zeros_like(trace_m)
    lift_m[...] = jnp.zeros_like(lift_m)
    for load in loads[:3]:
        load.wait()
    for first, ref in ((0, volume), (size_pad, face_minus), (size_pad + face_pad, face_plus)):
        high, low = split(ref[...])
        trace_m[0, first : first + ref.shape[0], :] = high
        trace_m[1, first : first + ref.shape[0], :] = low
    lane = lax.broadcasted_iota(jnp.int32, (face_pad, lines), 1)
    narrow = lax.broadcasted_iota(jnp.int32, (face_pad, halo_out.shape[2]), 1)

    def halo_copy(turn, side):
        slot = 2 * turn + side
        return pltpu.make_async_remote_copy(
            src_ref=halo_out.at[slot],
            dst_ref=halo_in.at[slot],
            send_sem=halo_send.at[slot],
            recv_sem=halo_recv.at[slot],
            device_id={"stream": left if side == 0 else right},
            device_id_type=MESH,
        )

    def start_rate(field, turn):
        first = jnp.zeros((face_pad, halo_out.shape[2]), F32)
        final = jnp.zeros((face_pad, halo_out.shape[2]), F32)
        for k in range(elements):
            out = product((trace_m[0], trace_m[1]), field(k))
            traces[k] = out
            low = out[size_pad : size_pad + face_pad]
            high = out[size_pad + face_pad :]
            first = jnp.where(narrow == k, low[:, :1], first)
            final = jnp.where(narrow == k, high[:, lines - 1 :], final)
        halo_out[2 * turn] = first
        halo_out[2 * turn + 1] = final
        halo_copy(turn, 0).start()
        halo_copy(turn, 1).start()

    def wait_rate(turn):
        halo_copy(turn, 0).wait()
        halo_copy(turn, 1).wait()

    def rate(k, turn):
        low = traces[k, size_pad : size_pad + face_pad, :]
        high = traces[k, size_pad + face_pad :, :]
        low_next = halo_in[2 * turn][:, k : k + 1]
        high_prev = halo_in[2 * turn + 1][:, k : k + 1]
        up = jnp.where(lane == lines - 1, low_next, pltpu.roll(low, lines - 1, 1)) - high
        down = low - jnp.where(lane == 0, high_prev, pltpu.roll(high, 1, 1))
        return (
            traces[k, :size, :]
            + product((lift_m[0, 0], lift_m[1, 0]), up)
            + product((lift_m[0, 1], lift_m[1, 1]), down)
        )


    def active(k):
        element = position * elements + k
        return ((begin <= element) & (element < end)).astype(F32)

    loads[3].wait()
    start_rate(lambda k: state[k], 0)
    for load in loads[4:]:
        load.wait()
    begin = offsets[...]
    end = begin + counts[...]
    for which, ref in ((0, lift_plus), (1, lift_minus)):
        high, low = split(ref[...].T)
        lift_m[0, which, :, :faces] = high
        lift_m[1, which, :, :faces] = low

    for k in range(elements):
        step = product(split(pivot_inv[k]), lower_block[k])
        put(step_m, k, step)
        put(upper_m, k, upper_block[k])
    spikes = [-(step_m[0, 0].astype(F32) + step_m[1, 0].astype(F32))]
    for k in range(1, elements):
        spikes.append(-product(take(step_m, k), spikes[-1]))
    put(exit_m, 0, spikes[-1])
    map_y, map_x = spikes[-1], -upper_block[elements - 1]
    put(reach_y, elements - 1, map_y)
    put(reach_x, elements - 1, map_x)
    for k in reversed(range(elements - 1)):
        map_y = spikes[k] - product(take(upper_m, k), map_y)
        map_x = -product(take(upper_m, k), map_x)
        put(reach_y, k, map_y)
        put(reach_x, k, map_x)

    def m_copy():
        return pltpu.make_async_remote_copy(
            src_ref=m_out,
            dst_ref=m_in,
            send_sem=m_send,
            recv_sem=m_recv,
            device_id={"wall": lax.rem(position + walls - 1, walls)},
            device_id_type=MESH,
        )

    @pl.when(position == walls - 1)
    def _():
        m_out[...] = map_y
        m_copy().start()

    wait_rate(0)
    local = None
    for k in range(elements):
        right_side = active(k) * (state[k] + section_step * rate(k, 0))
        forced = product(split(pivot_inv[k]), right_side)
        local = forced if k == 0 else forced - product(take(step_m, k), local)
        rows[k] = local

    def y_copy(c):
        return pltpu.make_async_remote_copy(
            src_ref=y_out.at[c],
            dst_ref=y_in.at[c],
            send_sem=y_send.at[c],
            recv_sem=y_recv.at[c],
            device_id={"wall": lax.rem(position + 1, walls)},
            device_id_type=MESH,
        )

    def x_copy(c):
        return pltpu.make_async_remote_copy(
            src_ref=x_out.at[c],
            dst_ref=x_in.at[c],
            send_sem=x_send.at[c],
            recv_sem=x_recv.at[c],
            device_id={"wall": lax.rem(position + walls - 1, walls)},
            device_id_type=MESH,
        )

    columns = [slice(c * width, (c + 1) * width) for c in range(chunks)]

    @pl.when(position == 0)
    def _():
        for c in range(chunks):
            y_out[c] = rows[elements - 1, :, columns[c]]
            y_copy(c).start()

    last[...] = rows[elements - 1]
    after = rows[elements - 1]
    for k in reversed(range(elements - 1)):
        after = rows[k] - product(take(upper_m, k), after)
        rows[k] = after

    @pl.when(position == walls - 1)
    def _():
        for c in range(chunks):
            x_out[c] = rows[0, :, columns[c]]
            x_copy(c).start()

    @pl.when(jnp.logical_and(position >= half, position < walls - 1))
    def _():
        m_copy().wait_recv()
        through = product(take(reach_x, 0), m_in[...])
        put(down_m, 0, through)
        m_out[...] = (reach_y[0, 0].astype(F32) + reach_y[1, 0].astype(F32)) + product(
            take(down_m, 0), spikes[-1]
        )
        m_copy().start()
        above = rows[0] + product(take(down_m, 0), last[...])
        for c in range(chunks):
            x_copy(c).wait_recv()
            x_out[c] = above[:, columns[c]] + product(take(reach_x, 0), x_in[c])
            x_copy(c).start()

    @pl.when(jnp.logical_and(position > 0, position < half))
    def _():
        for c in range(chunks):
            y_copy(c).wait_recv()
            y_out[c] = last[:, columns[c]] + product(take(exit_m, 0), y_in[c])
            y_copy(c).start()

    @pl.when(position >= half)
    def _():
        for c in range(chunks):
            y_copy(c).wait_recv()

            @pl.when(position < walls - 1)
            def _():
                y_out[c] = last[:, columns[c]] + product(take(exit_m, 0), y_in[c])
                y_copy(c).start()
                x_in[c] = x_in[c] + product(split(m_in[...]), y_out[c])

    @pl.when(position == half - 1)
    def _():
        m_copy().wait_recv()
        meets = [product(split(m_in[...]), y_out[c]) for c in range(chunks)]
        starts = [
            rows[0, :, columns[c]]
            + product(take(reach_y, 0), y_in[c])
            + product(take(reach_x, 0), meets[c])
            for c in range(chunks)
        ]
        for c in range(chunks):
            x_copy(c).wait_recv()

            @pl.when(position > 0)
            def _():
                x_out[c] = starts[c] + product(take(reach_x, 0), x_in[c])
                x_copy(c).start()

            x_in[c] = x_in[c] + meets[c]

    @pl.when(position > 0)
    def _():
        for c in range(chunks):
            for k in range(elements):
                rows[k, :, columns[c]] += product(take(reach_y, k), y_in[c])

    @pl.when(position < half - 1)
    def _():
        for c in range(chunks):
            x_copy(c).wait_recv()

            @pl.when(position > 0)
            def _():
                x_out[c] = rows[0, :, columns[c]] + product(take(reach_x, 0), x_in[c])
                x_copy(c).start()

    @pl.when(position < walls - 1)
    def _():
        for c in range(chunks):
            for k in range(elements):
                rows[k, :, columns[c]] += product(take(reach_x, k), x_in[c])

    def store(which, k):
        return pltpu.make_async_copy(
            (rows, state)[which].at[k],
            (state_out, rate_out)[which].at[k],
            store_sem.at[which, k],
        )

    for k in range(elements):
        rows[k] = active(k) * rows[k]

    start_rate(lambda k: rows[k], 1)
    for k in range(elements):
        store(0, k).start()

    @pl.when(position < walls - 1)
    def _():
        for c in range(chunks):
            y_copy(c).wait_send()

    @pl.when(position > 0)
    def _():
        for c in range(chunks):
            x_copy(c).wait_send()

    @pl.when(position >= half)
    def _():
        m_copy().wait_send()

    wait_rate(1)
    for k in range(elements):
        state[k] = active(k) * rate(k, 1)
        store(1, k).start()
    for which in range(2):
        for k in range(elements):
            store(which, k).wait()


def solution(mesh):
    walls, streams = mesh.shape["wall"], mesh.shape["stream"]

    def body(
        state,
        pivot_inv,
        lower_block,
        upper_block,
        volume,
        face_minus,
        face_plus,
        lift_minus,
        lift_plus,
        offsets,
        counts,
    ):
        elements, size, lines = state.shape
        faces = face_minus.shape[0]
        size_pad, face_pad = ceil_to(size, 16), ceil_to(faces, 16)
        chunks = 2 if lines % 256 == 0 else 1
        width = lines // chunks
        halo_width = ceil_to(elements, 128)
        hbm = pl.BlockSpec(memory_space=pltpu.HBM)
        operands = (
            state,
            pivot_inv,
            lower_block,
            upper_block,
            volume,
            face_minus,
            face_plus,
            lift_minus.T,
            lift_plus.T,
            offsets.reshape(1, lines),
            counts.reshape(1, lines),
        )
        return pl.pallas_call(
            functools.partial(kernel, walls, streams),
            out_shape=(jax.ShapeDtypeStruct(state.shape, F32),) * 2,
            in_specs=[hbm] * 11,
            out_specs=(hbm, hbm),
            scratch_shapes=[pltpu.VMEM(x.shape, x.dtype) for x in operands]
            + [
                pltpu.SemaphoreType.DMA((len(operands),)),
                pltpu.SemaphoreType.DMA((2, elements)),
                pltpu.VMEM((2, size_pad + 2 * face_pad, size), BF16),
                pltpu.VMEM((2, 2, size, face_pad), BF16),
                pltpu.VMEM((2, elements, size, size), BF16),
                pltpu.VMEM((2, elements, size, size), BF16),
                pltpu.VMEM((2, elements, size, size), BF16),
                pltpu.VMEM((2, elements, size, size), BF16),
                pltpu.VMEM((2, 1, size, size), BF16),
                pltpu.VMEM((elements, size_pad + 2 * face_pad, lines), F32),
                pltpu.VMEM((elements, size, lines), F32),
                pltpu.VMEM((4, face_pad, halo_width), F32),
                pltpu.VMEM((4, face_pad, halo_width), F32),
                pltpu.VMEM((chunks, size, width), F32),
                pltpu.VMEM((chunks, size, width), F32),
                pltpu.VMEM((chunks, size, width), F32),
                pltpu.VMEM((chunks, size, width), F32),
                pltpu.VMEM((size, lines), F32),
                pltpu.VMEM((size, size), F32),
                pltpu.VMEM((size, size), F32),
                pltpu.VMEM((2, 1, size, size), BF16),
                pltpu.SemaphoreType.DMA((4,)),
                pltpu.SemaphoreType.DMA((4,)),
                pltpu.SemaphoreType.DMA((chunks,)),
                pltpu.SemaphoreType.DMA((chunks,)),
                pltpu.SemaphoreType.DMA((chunks,)),
                pltpu.SemaphoreType.DMA((chunks,)),
                pltpu.SemaphoreType.DMA,
                pltpu.SemaphoreType.DMA,
            ],
            compiler_params=pltpu.CompilerParams(
                collective_id=0, has_side_effects=True, vmem_limit_bytes=67043328
            ),
        )(*operands)

    in_specs = (
        P("wall", None, "stream"),
        P("wall", None, None),
        P("wall", None, None),
        P("wall", None, None),
        P(),
        P(),
        P(),
        P(),
        P(),
        P("stream"),
        P("stream"),
    )
    out_specs = (P("wall", None, "stream"), P("wall", None, "stream"))
    return jax.shard_map(body, mesh=mesh, in_specs=in_specs, out_specs=out_specs, check_vma=False)
```

```python
import functools

import jax
import jax.numpy as jnp
from jax import lax
from jax.experimental import pallas as pl
from jax.experimental.pallas import tpu as pltpu
from jax.sharding import PartitionSpec as P

section_step = 0.4
MESH = pl.DeviceIdType.MESH
F32 = jnp.float32
BF16 = jnp.bfloat16


def ceil_to(size, unit):
    return (size + unit - 1) // unit * unit


def split(x):
    high = x.astype(BF16)
    return high, (x - high.astype(F32)).astype(BF16)


def dot(a, b):
    return jnp.dot(a, b, preferred_element_type=F32)


def product(matrix, x):
    high, low = matrix
    x_high, x_low = split(x)
    return dot(high, x_high) + (dot(low, x_high) + dot(high, x_low))


def kernel(
    walls,
    streams,
    state_hbm,
    pivot_hbm,
    lower_hbm,
    upper_hbm,
    volume_hbm,
    minus_hbm,
    plus_hbm,
    lift_minus_hbm,
    lift_plus_hbm,
    offsets_hbm,
    counts_hbm,
    state_out,
    rate_out,
    state,
    pivot_inv,
    lower_block,
    upper_block,
    volume,
    face_minus,
    face_plus,
    lift_minus,
    lift_plus,
    offsets,
    counts,
    load_sem,
    store_sem,
    trace_m,
    lift_m,
    step_m,
    upper_m,
    reach_y,
    reach_x,
    exit_m,
    traces,
    rows,
    halo_out,
    halo_in,
    y_out,
    y_in,
    x_out,
    x_in,
    last,
    exit_f,
    m_out,
    m_in,
    down_m,
    halo_send,
    halo_recv,
    y_send,
    y_recv,
    x_send,
    x_recv,
    m_send,
    m_recv,
):
    elements, size, lines = state.shape
    faces = face_minus.shape[0]
    size_pad, face_pad = ceil_to(size, 16), ceil_to(faces, 16)
    chunks = y_out.shape[0]
    width = lines // chunks
    position = lax.axis_index("wall")
    here = lax.axis_index("stream")
    right, left = lax.rem(here + 1, streams), lax.rem(here + streams - 1, streams)

    half = walls // 2
    sources = (
        (volume_hbm, volume),
        (minus_hbm, face_minus),
        (plus_hbm, face_plus),
        (state_hbm, state),
        (pivot_hbm, pivot_inv),
        (lower_hbm, lower_block),
        (upper_hbm, upper_block),
        (lift_minus_hbm, lift_minus),
        (lift_plus_hbm, lift_plus),
        (offsets_hbm, offsets),
        (counts_hbm, counts),
    )
    loads = [
        pltpu.make_async_copy(source, target, load_sem.at[i])
        for i, (source, target) in enumerate(sources)
    ]
    for load in loads:
        load.start()

    barrier = pltpu.get_barrier_semaphore()
    pl.semaphore_signal(barrier, inc=1, device_id={"stream": left}, device_id_type=MESH)
    pl.semaphore_signal(barrier, inc=1, device_id={"stream": right}, device_id_type=MESH)

    @pl.when(position > 0)
    def _():
        pl.semaphore_signal(barrier, inc=1, device_id={"wall": position - 1}, device_id_type=MESH)

    @pl.when(position < walls - 1)
    def _():
        pl.semaphore_signal(barrier, inc=1, device_id={"wall": position + 1}, device_id_type=MESH)

    inner = jnp.logical_and(position > 0, position < walls - 1)

    @pl.when(inner)
    def _():
        pl.semaphore_wait(barrier, 4)

    @pl.when(jnp.logical_not(inner))
    def _():
        pl.semaphore_wait(barrier, 3)

    def put(ref, index, value):
        high, low = split(value)
        ref[0, index] = high
        ref[1, index] = low

    def take(ref, index):
        return ref[0, index], ref[1, index]

    trace_m[...] = jnp.zeros_like(trace_m)
    lift_m[...] = jnp.zeros_like(lift_m)
    for load in loads[:3]:
        load.wait()
    for first, ref in ((0, volume), (size_pad, face_minus), (size_pad + face_pad, face_plus)):
        high, low = split(ref[...])
        trace_m[0, first : first + ref.shape[0], :] = high
        trace_m[1, first : first + ref.shape[0], :] = low
    lane = lax.broadcasted_iota(jnp.int32, (face_pad, lines), 1)
    narrow = lax.broadcasted_iota(jnp.int32, (face_pad, halo_out.shape[2]), 1)

    def halo_copy(turn, side):
        slot = 2 * turn + side
        return pltpu.make_async_remote_copy(
            src_ref=halo_out.at[slot],
            dst_ref=halo_in.at[slot],
            send_sem=halo_send.at[slot],
            recv_sem=halo_recv.at[slot],
            device_id={"stream": left if side == 0 else right},
            device_id_type=MESH,
        )

    def start_rate(field, turn):
        first = jnp.zeros((face_pad, halo_out.shape[2]), F32)
        final = jnp.zeros((face_pad, halo_out.shape[2]), F32)
        for k in range(elements):
            out = product((trace_m[0], trace_m[1]), field(k))
            traces[k] = out
            low = out[size_pad : size_pad + face_pad]
            high = out[size_pad + face_pad :]
            first = jnp.where(narrow == k, low[:, :1], first)
            final = jnp.where(narrow == k, high[:, lines - 1 :], final)
        halo_out[2 * turn] = first
        halo_out[2 * turn + 1] = final
        halo_copy(turn, 0).start()
        halo_copy(turn, 1).start()

    def wait_rate(turn):
        halo_copy(turn, 0).wait()
        halo_copy(turn, 1).wait()

    def rate(k, turn):
        low = traces[k, size_pad : size_pad + face_pad, :]
        high = traces[k, size_pad + face_pad :, :]
        low_next = halo_in[2 * turn][:, k : k + 1]
        high_prev = halo_in[2 * turn + 1][:, k : k + 1]
        up = jnp.where(lane == lines - 1, low_next, pltpu.roll(low, lines - 1, 1)) - high
        down = low - jnp.where(lane == 0, high_prev, pltpu.roll(high, 1, 1))
        return (
            traces[k, :size, :]
            + product((lift_m[0, 0], lift_m[1, 0]), up)
            + product((lift_m[0, 1], lift_m[1, 1]), down)
        )


    def active(k):
        element = position * elements + k
        return ((begin <= element) & (element < end)).astype(F32)

    loads[3].wait()
    start_rate(lambda k: state[k], 0)
    for load in loads[4:]:
        load.wait()
    begin = offsets[...]
    end = begin + counts[...]
    for which, ref in ((0, lift_plus), (1, lift_minus)):
        high, low = split(ref[...].T)
        lift_m[0, which, :, :faces] = high
        lift_m[1, which, :, :faces] = low

    for k in range(elements):
        step = product(split(pivot_inv[k]), lower_block[k])
        put(step_m, k, step)
        put(upper_m, k, upper_block[k])

    def form_spikes():
        spike = -(step_m[0, 0].astype(F32) + step_m[1, 0].astype(F32))
        put(reach_y, 0, spike)
        for k in range(1, elements):
            spike = -product(take(step_m, k), spike)
            put(reach_y, k, spike)
        exit_f[...] = spike
        put(exit_m, 0, spike)

    def form_reach():
        map_y, map_x = exit_f[...], -upper_block[elements - 1]
        put(reach_x, elements - 1, map_x)
        for k in reversed(range(elements - 1)):
            spike = reach_y[0, k].astype(F32) + reach_y[1, k].astype(F32)
            map_y = spike - product(take(upper_m, k), map_y)
            map_x = -product(take(upper_m, k), map_x)
            put(reach_y, k, map_y)
            put(reach_x, k, map_x)
        return map_y

    def m_copy():
        return pltpu.make_async_remote_copy(
            src_ref=m_out,
            dst_ref=m_in,
            send_sem=m_send,
            recv_sem=m_recv,
            device_id={"wall": lax.rem(position + walls - 1, walls)},
            device_id_type=MESH,
        )

    @pl.when(position >= half)
    def _():
        form_spikes()
        map_y = form_reach()

        @pl.when(position == walls - 1)
        def _():
            m_out[...] = map_y
            m_copy().start()

    wait_rate(0)
    local = None
    for k in range(elements):
        right_side = active(k) * (state[k] + section_step * rate(k, 0))
        forced = product(split(pivot_inv[k]), right_side)
        local = forced if k == 0 else forced - product(take(step_m, k), local)
        rows[k] = local

    def y_copy(c):
        return pltpu.make_async_remote_copy(
            src_ref=y_out.at[c],
            dst_ref=y_in.at[c],
            send_sem=y_send.at[c],
            recv_sem=y_recv.at[c],
            device_id={"wall": lax.rem(position + 1, walls)},
            device_id_type=MESH,
        )

    def x_copy(c):
        return pltpu.make_async_remote_copy(
            src_ref=x_out.at[c],
            dst_ref=x_in.at[c],
            send_sem=x_send.at[c],
            recv_sem=x_recv.at[c],
            device_id={"wall": lax.rem(position + walls - 1, walls)},
            device_id_type=MESH,
        )

    columns = [slice(c * width, (c + 1) * width) for c in range(chunks)]

    @pl.when(position == 0)
    def _():
        for c in range(chunks):
            y_out[c] = rows[elements - 1, :, columns[c]]
            y_copy(c).start()

    last[...] = rows[elements - 1]

    @pl.when(position < half)
    def _():
        form_spikes()

    @pl.when(jnp.logical_and(position >= half, position < walls - 1))
    def _():
        m_copy().wait_recv()
        put(down_m, 0, product(take(reach_x, 0), m_in[...]))
        m_out[...] = (reach_y[0, 0].astype(F32) + reach_y[1, 0].astype(F32)) + product(
            take(down_m, 0), exit_f[...]
        )
        m_copy().start()

    after = rows[elements - 1]
    for k in reversed(range(elements - 1)):
        after = rows[k] - product(take(upper_m, k), after)
        rows[k] = after

    @pl.when(position == walls - 1)
    def _():
        for c in range(chunks):
            x_out[c] = rows[0, :, columns[c]]
            x_copy(c).start()

    @pl.when(jnp.logical_and(position >= half, position < walls - 1))
    def _():
        above = rows[0] + product(take(down_m, 0), last[...])
        for c in range(chunks):
            x_copy(c).wait_recv()
            x_out[c] = above[:, columns[c]] + product(take(reach_x, 0), x_in[c])
            x_copy(c).start()

    @pl.when(jnp.logical_and(position > 0, position < half))
    def _():
        for c in range(chunks):
            y_copy(c).wait_recv()
            y_out[c] = last[:, columns[c]] + product(take(exit_m, 0), y_in[c])
            y_copy(c).start()

    @pl.when(position < half)
    def _():
        form_reach()

    @pl.when(position >= half)
    def _():
        for c in range(chunks):
            y_copy(c).wait_recv()

            @pl.when(position < walls - 1)
            def _():
                y_out[c] = last[:, columns[c]] + product(take(exit_m, 0), y_in[c])
                y_copy(c).start()
                x_in[c] = x_in[c] + product(split(m_in[...]), y_out[c])

    @pl.when(position == half - 1)
    def _():
        m_copy().wait_recv()
        meets = [product(split(m_in[...]), y_out[c]) for c in range(chunks)]
        starts = [
            rows[0, :, columns[c]]
            + product(take(reach_y, 0), y_in[c])
            + product(take(reach_x, 0), meets[c])
            for c in range(chunks)
        ]
        for c in range(chunks):
            x_copy(c).wait_recv()

            @pl.when(position > 0)
            def _():
                x_out[c] = starts[c] + product(take(reach_x, 0), x_in[c])
                x_copy(c).start()

            x_in[c] = x_in[c] + meets[c]

    @pl.when(position > 0)
    def _():
        for c in range(chunks):
            for k in range(elements):
                rows[k, :, columns[c]] += product(take(reach_y, k), y_in[c])

    @pl.when(position < half - 1)
    def _():
        for c in range(chunks):
            x_copy(c).wait_recv()

            @pl.when(position > 0)
            def _():
                x_out[c] = rows[0, :, columns[c]] + product(take(reach_x, 0), x_in[c])
                x_copy(c).start()

    @pl.when(position < walls - 1)
    def _():
        for c in range(chunks):
            for k in range(elements):
                rows[k, :, columns[c]] += product(take(reach_x, k), x_in[c])

    def store(which, k):
        return pltpu.make_async_copy(
            (rows, state)[which].at[k],
            (state_out, rate_out)[which].at[k],
            store_sem.at[which, k],
        )

    for k in range(elements):
        rows[k] = active(k) * rows[k]

    start_rate(lambda k: rows[k], 1)
    for k in range(elements):
        store(0, k).start()

    @pl.when(position < walls - 1)
    def _():
        for c in range(chunks):
            y_copy(c).wait_send()

    @pl.when(position > 0)
    def _():
        for c in range(chunks):
            x_copy(c).wait_send()

    @pl.when(position >= half)
    def _():
        m_copy().wait_send()

    wait_rate(1)
    for k in range(elements):
        state[k] = active(k) * rate(k, 1)
        store(1, k).start()
    for which in range(2):
        for k in range(elements):
            store(which, k).wait()


def solution(mesh):
    walls, streams = mesh.shape["wall"], mesh.shape["stream"]

    def body(
        state,
        pivot_inv,
        lower_block,
        upper_block,
        volume,
        face_minus,
        face_plus,
        lift_minus,
        lift_plus,
        offsets,
        counts,
    ):
        elements, size, lines = state.shape
        faces = face_minus.shape[0]
        size_pad, face_pad = ceil_to(size, 16), ceil_to(faces, 16)
        chunks = 2 if lines % 256 == 0 else 1
        width = lines // chunks
        halo_width = ceil_to(elements, 128)
        hbm = pl.BlockSpec(memory_space=pltpu.HBM)
        operands = (
            state,
            pivot_inv,
            lower_block,
            upper_block,
            volume,
            face_minus,
            face_plus,
            lift_minus.T,
            lift_plus.T,
            offsets.reshape(1, lines),
            counts.reshape(1, lines),
        )
        return pl.pallas_call(
            functools.partial(kernel, walls, streams),
            out_shape=(jax.ShapeDtypeStruct(state.shape, F32),) * 2,
            in_specs=[hbm] * 11,
            out_specs=(hbm, hbm),
            scratch_shapes=[pltpu.VMEM(x.shape, x.dtype) for x in operands]
            + [
                pltpu.SemaphoreType.DMA((len(operands),)),
                pltpu.SemaphoreType.DMA((2, elements)),
                pltpu.VMEM((2, size_pad + 2 * face_pad, size), BF16),
                pltpu.VMEM((2, 2, size, face_pad), BF16),
                pltpu.VMEM((2, elements, size, size), BF16),
                pltpu.VMEM((2, elements, size, size), BF16),
                pltpu.VMEM((2, elements, size, size), BF16),
                pltpu.VMEM((2, elements, size, size), BF16),
                pltpu.VMEM((2, 1, size, size), BF16),
                pltpu.VMEM((elements, size_pad + 2 * face_pad, lines), F32),
                pltpu.VMEM((elements, size, lines), F32),
                pltpu.VMEM((4, face_pad, halo_width), F32),
                pltpu.VMEM((4, face_pad, halo_width), F32),
                pltpu.VMEM((chunks, size, width), F32),
                pltpu.VMEM((chunks, size, width), F32),
                pltpu.VMEM((chunks, size, width), F32),
                pltpu.VMEM((chunks, size, width), F32),
                pltpu.VMEM((size, lines), F32),
                pltpu.VMEM((size, size), F32),
                pltpu.VMEM((size, size), F32),
                pltpu.VMEM((size, size), F32),
                pltpu.VMEM((2, 1, size, size), BF16),
                pltpu.SemaphoreType.DMA((4,)),
                pltpu.SemaphoreType.DMA((4,)),
                pltpu.SemaphoreType.DMA((chunks,)),
                pltpu.SemaphoreType.DMA((chunks,)),
                pltpu.SemaphoreType.DMA((chunks,)),
                pltpu.SemaphoreType.DMA((chunks,)),
                pltpu.SemaphoreType.DMA,
                pltpu.SemaphoreType.DMA,
            ],
            compiler_params=pltpu.CompilerParams(
                collective_id=0, has_side_effects=True, vmem_limit_bytes=67043328
            ),
        )(*operands)

    in_specs = (
        P("wall", None, "stream"),
        P("wall", None, None),
        P("wall", None, None),
        P("wall", None, None),
        P(),
        P(),
        P(),
        P(),
        P(),
        P("stream"),
        P("stream"),
    )
    out_specs = (P("wall", None, "stream"), P("wall", None, "stream"))
    return jax.shard_map(body, mesh=mesh, in_specs=in_specs, out_specs=out_specs, check_vma=False)
```
